32 devices in a mesh: party: 2 (over x), dp: 16 (over z, y, core).
Axes of the slice: x: 2, y: 2, z: 4, core: 2. Of those that a mesh axis runs over, the one named last changes fastest.
Arguments:
- x_share: float32 [2, 8192, 1024], P('party', 'dp'), may hold values from -6 to 6
- w_share: float32 [2, 1024, 2048], P('party', 'dp'), may hold values from -0.1875 to 0.1875
- g_share: float32 [2, 8192, 2048], P('party', 'dp'), may hold values from -0.0625 to 0.0625
- fwd_a: float32 [2, 8192, 1024], P('party', 'dp'), may hold values from -4 to 4
- fwd_b: float32 [2, 1024, 2048], P('party', 'dp'), may hold values from -0.125 to 0.125
- fwd_c: float32 [2, 8192, 2048], P('party', 'dp'), may hold values from -2100 to 2100, as said below
- bwd_a: float32 [2, 8192, 1024], P('party', 'dp'), may hold values from -4 to 4
- bwd_b: float32 [2, 8192, 2048], P('party', 'dp'), may hold values from -0.044194174 to 0.044194174
- bwd_c: float32 [2, 1024, 2048], P('party', 'dp'), may hold values from -2100 to 2100, as said below
Outputs:
- y_share: float32 [2, 8192, 2048], P('party', 'dp')
- dw_share: float32 [2, 1024, 2048], P('party', 'dp')
The draws below stay inside these ranges and needn't reach their ends.
Inputs may be any that keep to these rules, and one draw needn't show every extreme that they name: fwd_c[0] + fwd_c[1] equals (fwd_a[0] + fwd_a[1]) (fwd_b[0] + fwd_b[1]) up to float32 rounding. bwd_c[0] + bwd_c[1] equals (bwd_a[0] + bwd_a[1])^T (bwd_b[0] + bwd_b[1]) up to float32 rounding.
All inputs are finite; a program needn't handle non-finite values.
Results may differ from the reference program's by a relative error of at most 0.0001.
Values sent between devices are 32-bit elements; how exact they have to be, the bound alone decides.
A program may use at most 128 MiB of HBM per device.

```python
import jax
import jax.numpy as jnp
from jax import lax

D = 1024
FF = 2048
TOKENS = 8192


def factor_left(key, salt):
    return jnp.clip(jax.random.normal(jax.random.fold_in(key, salt), (2, TOKENS, D), jnp.float32), -4.0, 4.0)


def forward_right(key):
    values = jnp.clip(jax.random.normal(jax.random.fold_in(key, 21), (2, D, FF), jnp.float32), -4.0, 4.0)
    return values * (1.0 / 32.0)


def backward_right(key):
    values = jnp.clip(jax.random.normal(jax.random.fold_in(key, 31), (2, TOKENS, FF), jnp.float32), -4.0, 4.0)
    return values * (1.0 / TOKENS) ** 0.5


def draw_fwd_a(key, part):
    return factor_left(key, 11)


def draw_fwd_b(key, part):
    return forward_right(key)


def draw_fwd_c(key, part):
    left = factor_left(key, 11)
    right = forward_right(key)
    product = jnp.dot(left[0] + left[1], right[0] + right[1], precision=lax.Precision.HIGHEST, preferred_element_type=jnp.float32)
    masking = jnp.clip(jax.random.normal(jax.random.fold_in(key, 41), (TOKENS, FF), jnp.float32), -4.0, 4.0)
    return jnp.stack([product - masking, masking])


def draw_bwd_a(key, part):
    return factor_left(key, 13)


def draw_bwd_b(key, part):
    return backward_right(key)


def draw_bwd_c(key, part):
    left = factor_left(key, 13)
    right = backward_right(key)
    product = lax.dot_general(left[0] + left[1], right[0] + right[1], (((0,), (0,)), ((), ())), precision=lax.Precision.HIGHEST, preferred_element_type=jnp.float32)
    masking = jnp.clip(jax.random.normal(jax.random.fold_in(key, 43), (D, FF), jnp.float32), -4.0, 4.0)
    return jnp.stack([product - masking, masking])


def steps_of(rng, dims, cuts, smallest, largest):
    level = 1.0
    for dim, parts in cuts:
        draws = jax.random.uniform(jax.random.fold_in(jax.random.fold_in(rng, 6), dim), (parts,), jnp.float32, smallest / len(cuts), largest / len(cuts))
        level = level * jnp.repeat(jnp.exp(draws), dims[dim] // parts).reshape((-1,) + (1,) * (len(dims) - 1 - dim))
    return level


def noise(stream_key, extent, scale, limit, shards=(), held_as=jnp.bfloat16):
    level = steps_of(stream_key, extent, shards, -0.22, 0.18) if shards else 1.0
    drawn = jax.random.normal(stream_key, extent, jnp.float32) * scale * level
    return jnp.minimum(jnp.maximum(drawn, -limit), limit).astype(held_as)


def setup_inputs(seed: int = 0) -> dict:
    key_of = jax.random.split(jax.random.key(seed), 10)
    return {
        "x_share": noise(key_of[0], (2, TOKENS, D), 1.0, 6.0, ((0, 2), (1, 16)), jnp.float32),
        "w_share": noise(key_of[1], (2, D, FF), D ** -0.5, 0.1875, ((0, 2), (1, 16)), jnp.float32),
        "g_share": noise(key_of[2], (2, TOKENS, FF), TOKENS ** -0.5, 0.0625, ((0, 2), (1, 16)), jnp.float32),
        "fwd_a": draw_fwd_a(jax.random.fold_in(key_of[9], 71), 0),
        "fwd_b": draw_fwd_b(jax.random.fold_in(key_of[9], 71), 0),
        "fwd_c": draw_fwd_c(jax.random.fold_in(key_of[9], 71), 0),
        "bwd_a": draw_bwd_a(jax.random.fold_in(key_of[9], 71), 0),
        "bwd_b": draw_bwd_b(jax.random.fold_in(key_of[9], 71), 0),
        "bwd_c": draw_bwd_c(jax.random.fold_in(key_of[9], 71), 0),
    }


def matmul(left, right):
    return jnp.dot(left, right, preferred_element_type=jnp.float32, precision=lax.Precision.HIGHEST)


def tmatmul(left, right):
    return lax.dot_general(left, right, (((0,), (0,)), ((), ())), precision=lax.Precision.HIGHEST, preferred_element_type=jnp.float32)


def reference(x_share, w_share, g_share, fwd_a, fwd_b, fwd_c, bwd_a, bwd_b, bwd_c):
    eps_fwd = (x_share[0] - fwd_a[0]) + (x_share[1] - fwd_a[1])
    delta_fwd = (w_share[0] - fwd_b[0]) + (w_share[1] - fwd_b[1])
    eps_bwd = (x_share[0] - bwd_a[0]) + (x_share[1] - bwd_a[1])
    delta_bwd = (g_share[0] - bwd_b[0]) + (g_share[1] - bwd_b[1])
    outputs = []
    grads = []
    for party in range(2):
        first = jnp.float32(1.0 if party == 0 else 0.0)
        outputs.append(fwd_c[party] + matmul(eps_fwd, fwd_b[party] + first * delta_fwd) + matmul(fwd_a[party], delta_fwd))
        grads.append(bwd_c[party] + tmatmul(eps_bwd, bwd_b[party] + first * delta_bwd) + tmatmul(bwd_a[party], delta_bwd))
    return jnp.stack(outputs), jnp.stack(grads)
```

```python
import jax
import jax.numpy as jnp
from jax import lax
from jax.sharding import PartitionSpec as P


def matmul(left, right):
    return jnp.dot(left, right, preferred_element_type=jnp.float32, precision=lax.Precision.HIGH)


def tmatmul(left, right):
    return lax.dot_general(
        left,
        right,
        (((0,), (0,)), ((), ())),
        precision=lax.Precision.HIGH,
        preferred_element_type=jnp.float32,
    )


def swap(value):
    return lax.ppermute(value, "party", [(0, 1), (1, 0)])


def body(x_share, w_share, g_share, fwd_a, fwd_b, fwd_c, bwd_a, bwd_b, bwd_c):
    first = (lax.axis_index("party") == 0).astype(jnp.float32)
    inputs, a_f, b_f, a_b, b_b = x_share[0], fwd_a[0], fwd_b[0], bwd_a[0], bwd_b[0]
    own_w = w_share[0] - b_f
    gathered_b = lax.all_gather(b_f, "dp", axis=0, tiled=True)
    got_w = swap(own_w)
    delta_fwd = lax.all_gather(own_w + got_w, "dp", axis=0, tiled=True)
    own_e, own_d = inputs - a_b, g_share[0] - b_b
    got_e = swap(own_e)
    got_d = swap(own_d)
    own_f = inputs - a_f
    got_f = swap(own_f)
    eps_bwd, delta_bwd = own_e + got_e, own_d + got_d
    partial_value = tmatmul(eps_bwd, b_b) + tmatmul(a_b + first * eps_bwd, delta_bwd)
    summed = lax.psum_scatter(partial_value, "dp", scatter_dimension=0, tiled=True)
    eps_fwd = own_f + got_f
    outputs = fwd_c[0] + matmul(eps_fwd, gathered_b) + matmul(a_f + first * eps_fwd, delta_fwd)
    return (outputs[None], (bwd_c[0] + summed)[None])


def solution(mesh):
    spec = P("party", "dp", None)
    return jax.shard_map(body, mesh=mesh, in_specs=(spec,) * 9, out_specs=(spec, spec), check_vma=False)
```

```python
import functools

import jax
import jax.numpy as jnp
from jax import lax
from jax.experimental import pallas as pl
from jax.experimental.pallas import tpu as pltpu
from jax.sharding import PartitionSpec as P

MESH = pl.DeviceIdType.MESH
STREAMS = 4


def place(index, n):
    z, y, core = index // 4, (index // 2) % 2, index % 2
    return 2 * (z + y * (n // 2 - 1 - 2 * z)) + core


def index_at(spot, n):
    chip, core = spot // 2, spot % 2
    y = chip // (n // 4)
    z = chip + y * (n // 2 - 1 - 2 * chip)
    return 4 * z + 2 * y + core


def scatter_kernel(n, part_ref, base_ref, out_ref, own, slots, load_sem, send_sem, recv_sem):
    me = place(lax.axis_index("dp"), n)
    after, before = index_at(lax.rem(me + 1, n), n), index_at(lax.rem(me + n - 1, n), n)
    rows, columns = base_ref.shape
    width = columns // STREAMS
    load = pltpu.make_async_copy(part_ref, own, load_sem)
    load.start()
    barrier = pltpu.get_barrier_semaphore()
    for neighbour in (after, before):
        pl.semaphore_signal(barrier, inc=1, device_id={"dp": neighbour}, device_id_type=MESH)
    pl.semaphore_wait(barrier, 2)
    load.wait()

    def rows_of(sign, step):
        owner = index_at(lax.rem(me + sign * (n - 1 - step) + n * 2, n), n)
        return pl.ds(pl.multiple_of(owner * rows, 8), rows)

    def copy_of(stream, step, source):
        target = after if stream % 2 == 0 else before
        return pltpu.make_async_remote_copy(
            src_ref=source,
            dst_ref=slots.at[stream, step],
            send_sem=send_sem.at[stream, step],
            recv_sem=recv_sem.at[stream, step],
            device_id={"dp": target},
            device_id_type=MESH,
        )

    def sign_of(stream):
        return 1 if stream % 2 == 0 else -1

    def first_source(stream):
        return own.at[rows_of(sign_of(stream), 0), pl.ds(stream * width, width)]

    for stream in range(STREAMS):
        copy_of(stream, 0, first_source(stream)).start()

    def hop(step, carry):
        for stream in range(STREAMS):
            copy_of(stream, step - 1, slots.at[stream, step - 1]).wait_recv()
            slots[stream, step - 1] = slots[stream, step - 1] + own[rows_of(sign_of(stream), step), pl.ds(stream * width, width)]
            copy_of(stream, step, slots.at[stream, step - 1]).start()
        return carry

    lax.fori_loop(1, n - 1, hop, 0)
    for stream in range(STREAMS):
        cols = pl.ds(stream * width, width)
        copy_of(stream, n - 2, slots.at[stream, n - 2]).wait_recv()
        out_ref[:, cols] = base_ref[:, cols] + (slots[stream, n - 2] + own[rows_of(sign_of(stream), n - 1), cols])

    def drain(step, carry):
        for stream in range(STREAMS):
            copy_of(stream, step, slots.at[stream, step]).wait_send()
        return carry

    lax.fori_loop(0, n - 1, drain, 0)


def scatter_sum(part, base, n, number):
    rows, columns = base.shape
    return pl.pallas_call(
        functools.partial(scatter_kernel, n),
        out_shape=jax.ShapeDtypeStruct(base.shape, base.dtype),
        in_specs=[pl.BlockSpec(memory_space=pl.ANY), pl.BlockSpec(memory_space=pltpu.VMEM)],
        out_specs=pl.BlockSpec(memory_space=pltpu.VMEM),
        scratch_shapes=[
            pltpu.VMEM(part.shape, part.dtype),
            pltpu.VMEM((STREAMS, n - 1, rows, columns // STREAMS), part.dtype),
            pltpu.SemaphoreType.DMA,
            pltpu.SemaphoreType.DMA((STREAMS, n - 1)),
            pltpu.SemaphoreType.DMA((STREAMS, n - 1)),
        ],
        compiler_params=pltpu.CompilerParams(
            collective_id=number, has_side_effects=True, vmem_limit_bytes=40 * 1024 * 1024
        ),
        cost_estimate=pl.CostEstimate(flops=0, bytes_accessed=80 * 1024 * 1024, transcendentals=0),
    )(part, base)


def matmul(left, right):
    return jnp.dot(left, right, preferred_element_type=jnp.float32, precision=lax.Precision.HIGH)


def tmatmul(left, right):
    return lax.dot_general(
        left,
        right,
        (((0,), (0,)), ((), ())),
        precision=lax.Precision.HIGH,
        preferred_element_type=jnp.float32,
    )


def swap(value):
    return lax.ppermute(value, "party", [(0, 1), (1, 0)])


CUTS = 2


def body(n, x_share, w_share, g_share, fwd_a, fwd_b, fwd_c, bwd_a, bwd_b, bwd_c):
    first = (lax.axis_index("party") == 0).astype(jnp.float32)
    inputs, a_f, b_f, a_b, b_b = x_share[0], fwd_a[0], fwd_b[0], bwd_a[0], bwd_b[0]
    own_w = w_share[0] - b_f
    gathered_b = lax.all_gather(b_f, "dp", axis=0, tiled=True)
    got_w = swap(own_w)
    delta_fwd = lax.all_gather(own_w + got_w, "dp", axis=0, tiled=True)
    own_e = inputs - a_b
    got_e = swap(own_e)
    width = b_b.shape[1] // CUTS
    cuts = [slice(i * width, (i + 1) * width) for i in range(CUTS)]
    own_d = [g_share[0, :, c] - b_b[:, c] for c in cuts]
    got_d = [swap(d) for d in own_d]
    own_f = inputs - a_f
    half = own_f.shape[0] // 2
    got_f = [swap(own_f[:half]), swap(own_f[half:])]
    eps_bwd = own_e + got_e
    right = a_b + first * eps_bwd
    grads = []
    for i, c in enumerate(cuts):
        part = tmatmul(eps_bwd, b_b[:, c]) + tmatmul(right, own_d[i] + got_d[i])
        grads.append(scatter_sum(part, bwd_c[0, :, c], n, i))
    outputs = []
    for i, r in enumerate((slice(0, half), slice(half, None))):
        eps_fwd = own_f[r] + got_f[i]
        outputs.append(fwd_c[0, r] + matmul(eps_fwd, gathered_b) + matmul(a_f[r] + first * eps_fwd, delta_fwd))
    return (jnp.concatenate(outputs)[None], jnp.concatenate(grads, axis=1)[None])


def solution(mesh):
    spec = P("party", "dp", None)
    return jax.shard_map(
        functools.partial(body, mesh.shape["dp"]),
        mesh=mesh,
        in_specs=(spec,) * 9,
        out_specs=(spec, spec),
        check_vma=False,
    )
```

```python
import functools

import jax
import jax.numpy as jnp
from jax import lax
from jax.experimental import pallas as pl
from jax.experimental.pallas import tpu as pltpu
from jax.sharding import PartitionSpec as P


MESH = pl.DeviceIdType.MESH


def place(index, n):
    z, y, core = index // 4, (index // 2) % 2, index % 2
    return 2 * (z + y * (n // 2 - 1 - 2 * z)) + core


def index_at(spot, n):
    chip, core = spot // 2, spot % 2
    y = chip // (n // 4)
    z = chip + y * (n // 2 - 1 - 2 * chip)
    return 4 * z + 2 * y + core


def gather_kernel(n, own_ref, out_ref, keep_sem, send_sem, recv_sem):
    me = place(lax.axis_index("dp"), n)
    after, before = index_at(lax.rem(me + 1, n), n), index_at(lax.rem(me + n - 1, n), n)
    rows, columns = own_ref.shape
    width = columns // 2
    barrier = pltpu.get_barrier_semaphore()
    for neighbour in (after, before):
        pl.semaphore_signal(barrier, inc=1, device_id={"dp": neighbour}, device_id_type=MESH)
    pl.semaphore_wait(barrier, 2)

    def rows_of(sign, step):
        owner = index_at(lax.rem(me - sign * step + n, n), n)
        return pl.ds(pl.multiple_of(owner * rows, 8), rows)

    def copy_of(stream, step, start=False):
        sign = 1 if stream < 2 else -1
        cols = pl.ds((stream % 2) * width, width)
        here = out_ref.at[rows_of(sign, step), cols]
        return pltpu.make_async_remote_copy(
            src_ref=own_ref.at[:, cols] if start else here,
            dst_ref=here,
            send_sem=send_sem.at[stream, step],
            recv_sem=recv_sem.at[stream, step],
            device_id={"dp": after if stream < 2 else before},
            device_id_type=MESH,
        )

    def arrived(stream, step):
        sign = 1 if stream < 2 else -1
        cols = pl.ds((stream % 2) * width, width)
        here = out_ref.at[rows_of(sign, step + 1), cols]
        pltpu.make_async_remote_copy(
            src_ref=here,
            dst_ref=here,
            send_sem=send_sem.at[stream, step],
            recv_sem=recv_sem.at[stream, step],
            device_id={"dp": after if stream < 2 else before},
            device_id_type=MESH,
        ).wait_recv()

    up, down = n // 2, n - 1 - n // 2
    order = (0, 2, 1, 3)
    for stream in order:
        copy_of(stream, 0, True).start()
    keep = pltpu.make_async_copy(own_ref, out_ref.at[rows_of(1, 0)], keep_sem)
    keep.start()

    def hop(step, carry):
        for stream in order:
            arrived(stream, step - 1)
            copy_of(stream, step).start()
        return carry

    lax.fori_loop(1, down, hop, 0)
    for stream in (0, 1):
        arrived(stream, up - 2)
        copy_of(stream, up - 1).start()
    for stream in (2, 3):
        arrived(stream, down - 1)
    for stream in (0, 1):
        arrived(stream, up - 1)
    keep.wait()
    for stream in order:
        copy_of(stream, 0, True).wait_send()

    def drain(step, carry):
        for stream in order:
            copy_of(stream, step).wait_send()
        return carry

    lax.fori_loop(1, down, drain, 0)
    for stream in (0, 1):
        copy_of(stream, up - 1).wait_send()


def gather(own, n):
    rows, columns = own.shape
    return pl.pallas_call(
        functools.partial(gather_kernel, n),
        out_shape=jax.ShapeDtypeStruct((n * rows, columns), own.dtype),
        in_specs=[pl.BlockSpec(memory_space=pltpu.VMEM)],
        out_specs=pl.BlockSpec(memory_space=pl.ANY),
        scratch_shapes=[
            pltpu.SemaphoreType.DMA,
            pltpu.SemaphoreType.DMA((4, n // 2)),
            pltpu.SemaphoreType.DMA((4, n // 2)),
        ],
        compiler_params=pltpu.CompilerParams(
            collective_id=0, has_side_effects=True, vmem_limit_bytes=8 * 1024 * 1024
        ),
        cost_estimate=pl.CostEstimate(flops=0, bytes_accessed=160 * 1024 * 1024, transcendentals=0),
    )(own)


def matmul(left, right):
    return jnp.dot(left, right, preferred_element_type=jnp.float32, precision=lax.Precision.HIGH)


def tmatmul(left, right):
    return lax.dot_general(
        left,
        right,
        (((0,), (0,)), ((), ())),
        precision=lax.Precision.HIGH,
        preferred_element_type=jnp.float32,
    )


def swap(value):
    return lax.ppermute(value, "party", [(0, 1), (1, 0)])


CUTS = 4


def body(n, x_share, w_share, g_share, fwd_a, fwd_b, fwd_c, bwd_a, bwd_b, bwd_c):
    first = (lax.axis_index("party") == 0).astype(jnp.float32)
    inputs, a_f, b_f, a_b, b_b = x_share[0], fwd_a[0], fwd_b[0], bwd_a[0], bwd_b[0]
    own_w = w_share[0] - b_f
    gathered_b = lax.all_gather(b_f, "dp", axis=0, tiled=True)
    got_w = swap(own_w)
    delta_fwd = gather(own_w + got_w, n)
    own_e = inputs - a_b
    got_e = swap(own_e)
    width = b_b.shape[1] // CUTS
    cuts = [slice(i * width, (i + 1) * width) for i in range(CUTS)]
    own_d = [g_share[0, :, c] - b_b[:, c] for c in cuts]
    got_d = [swap(d) for d in own_d]
    own_f = inputs - a_f
    got_f = swap(own_f)
    own_e, delta_fwd = lax.optimization_barrier((own_e, delta_fwd))
    eps_bwd = own_e + got_e
    right = a_b + first * eps_bwd
    grads = []
    for i, c in enumerate(cuts):
        part = tmatmul(eps_bwd, b_b[:, c]) + tmatmul(right, own_d[i] + got_d[i])
        summed = lax.psum_scatter(part, "dp", scatter_dimension=0, tiled=True)
        grads.append(bwd_c[0, :, c] + summed)
    eps_fwd = own_f + got_f
    outputs = fwd_c[0] + matmul(eps_fwd, gathered_b) + matmul(a_f + first * eps_fwd, delta_fwd)
    return (outputs[None], jnp.concatenate(grads, axis=1)[None])


def solution(mesh):
    spec = P("party", "dp", None)
    return jax.shard_map(
        functools.partial(body, mesh.shape["dp"]),
        mesh=mesh,
        in_specs=(spec,) * 9,
        out_specs=(spec, spec),
        check_vma=False,
    )
```
